256 devices in a mesh: space: 16 (over x, y_lo, core), tm: 16 (over z, y_hi).
Axes of the slice: x: 4, y: 4 (y_hi: 2, y_lo: 2; y = y_hi * 2 + y_lo), z: 8, core: 2. Of those that a mesh axis runs over, the one named last changes fastest.
Arguments:
- velocity: bfloat16 [8192, 32768], P('space', 'tm'), may hold values from -6 to 6
- pressure_modes: bfloat16 [32768, 1024], P('tm'), may hold values from -6 to 6
- partner: int32 [8192], P('space'), may hold values from 0 to 8191, as said below
- counts: int32 [16], P('tm'), may hold values from 2048 to 31744, as said below
Outputs:
- residual: bfloat16 [8192, 32768], P('space', 'tm')
The draws below stay inside these ranges and needn't reach their ends.
Inputs may be any that keep to these rules, and one draw needn't show every extreme that they name: partner pairs each row of the rows of space index s with a row of space index s + 8 or s - 8, one to one, and partner[partner[r]] = r. counts[j] lies between max(j, 1) * 2048 and max(j, 1) * 2048 + 2048 / 2.
All inputs are finite; a program needn't handle non-finite values.
Results may differ from the reference program's by a relative error of at most 0.0034.
Values may be sent and summed in bfloat16 or wider, within the bound.
A program may use at most 64 MiB of HBM per device.

```python
import jax
import jax.numpy as jnp
from jax import lax

ROW_DEV = 512
TIME_DEV = 2048
MODES = 1024
ROWS = 8192
TIMES = 32768
N_TM = 16


def draw_partner(key, part):
    shards = ROWS // ROW_DEV
    half_shards = shards // 2
    split_keys = jax.random.split(key, half_shards)
    shuffles = jax.vmap(lambda k: jax.random.permutation(k, ROW_DEV))(split_keys).astype(jnp.int32)
    lower_rows = jnp.arange(half_shards * ROW_DEV, dtype=jnp.int32).reshape(half_shards, ROW_DEV)
    upper_rows = (jnp.arange(half_shards, dtype=jnp.int32)[:, None] + half_shards) * ROW_DEV + shuffles
    table = jnp.zeros((ROWS,), jnp.int32)
    table = table.at[lower_rows.reshape(-1)].set(upper_rows.reshape(-1))
    table = table.at[upper_rows.reshape(-1)].set(lower_rows.reshape(-1))
    return table


def draw_counts(key, part):
    shards = TIMES // TIME_DEV
    block_index = jnp.arange(shards, dtype=jnp.int32)
    extra = jax.random.randint(key, (shards,), 0, TIME_DEV // 2 + 1, dtype=jnp.int32)
    extra = extra.at[0].set(0)
    extra = extra.at[shards - 1].set(TIME_DEV // 2)
    return jnp.maximum(block_index, 1) * TIME_DEV + extra


def levels(rng, extent, cuts, least, largest):
    def one(axis_at, shards_of):
        draws = jax.random.uniform(jax.random.fold_in(jax.random.fold_in(rng, 6), axis_at), (shards_of,), jnp.float32, least / len(cuts), largest / len(cuts))
        return jnp.repeat(jnp.exp(draws), extent[axis_at] // shards_of).reshape((-1,) + (1,) * (len(extent) - axis_at - 1))

    factor_of = one(*cuts[0])
    for cut in cuts[1:]:
        factor_of = factor_of * one(*cut)
    return factor_of


def noise(rng, extent, deviation, reach, pieces=(), kind=jnp.bfloat16):
    drawn = deviation * jax.random.normal(rng, extent, jnp.float32)
    if pieces:
        drawn = drawn * levels(rng, extent, pieces, -0.22, 0.18)
    return jnp.clip(drawn, -reach, reach).astype(kind)


def setup_inputs(seed: int = 0) -> dict:
    splits = jax.random.split(jax.random.key(seed), 5)
    return {
        "velocity": noise(splits[0], (ROWS, TIMES), 1.0, 6.0, ((0, 16), (1, 16))),
        "pressure_modes": noise(splits[1], (TIMES, MODES), 1.0, 6.0, ((0, 16),)),
        "partner": draw_partner(jax.random.fold_in(splits[4], 71), 0),
        "counts": draw_counts(jax.random.fold_in(splits[4], 71), 0),
    }


def reference(velocity, pressure_modes, partner, counts):
    total_rows = velocity.shape[0]
    half_rows = total_rows // 2
    half_modes = pressure_modes.shape[1] // 2
    is_lower = (jnp.arange(total_rows) < half_rows)[:, None]
    contract = (((1,), (1,)), ((), ()))

    def by_parity(rows, sym_modes, anti_modes):
        lower = jnp.dot(rows[:half_rows], sym_modes, preferred_element_type=jnp.float32)
        upper = jnp.dot(rows[half_rows:], anti_modes, preferred_element_type=jnp.float32)
        return jnp.concatenate([lower, upper], axis=0)

    def one_block(prior_sum, block_index):
        start = (block_index * TIME_DEV).astype(jnp.int32)
        block = lax.dynamic_slice_in_dim(velocity, start, TIME_DEV, 1)
        mode_block = lax.dynamic_slice_in_dim(pressure_modes, start, TIME_DEV, 0)
        sym_modes = mode_block[:, :half_modes]
        anti_modes = mode_block[:, half_modes:]
        own_rows = block.astype(jnp.float32)
        partner_block = jnp.take(block, partner, axis=0)
        scaled = (prior_sum / counts[block_index].astype(jnp.float32)).astype(jnp.bfloat16)
        pred_lower = lax.dot_general(scaled[:half_rows], sym_modes, contract, preferred_element_type=jnp.float32)
        pred_upper = lax.dot_general(scaled[half_rows:], anti_modes, contract, preferred_element_type=jnp.float32)
        predicted = jnp.concatenate([pred_lower, pred_upper], axis=0).astype(jnp.bfloat16)
        own_pred = predicted.astype(jnp.float32)
        partner_pred = jnp.take(predicted, partner, axis=0).astype(jnp.float32)
        combined = jnp.where(is_lower, partner_pred + own_pred, partner_pred - own_pred)
        residual = (own_rows - combined).astype(jnp.bfloat16)
        mine = by_parity(block, sym_modes, anti_modes)
        theirs = by_parity(partner_block, sym_modes, anti_modes)
        correlation = jnp.where(is_lower, 0.5 * (theirs + mine), 0.5 * (theirs - mine))
        return prior_sum + correlation, residual

    start_sum = jnp.zeros((total_rows, half_modes), jnp.float32)
    _, blocks = lax.scan(one_block, start_sum, jnp.arange(N_TM, dtype=jnp.int32))
    return jnp.moveaxis(blocks, 0, 1).reshape(total_rows, N_TM * TIME_DEV)
```

```python
import functools

import jax
import jax.numpy as jnp
from jax import lax
from jax.experimental import pallas as pl
from jax.experimental.pallas import tpu as pltpu
from jax.sharding import PartitionSpec as P

MESH = pl.DeviceIdType.MESH
F32, BF16 = jnp.float32, jnp.bfloat16
CHUNKS = 4
TILE = 256
CONTRACT_LAST = (((1,), (1,)), ((), ()))


def kernel(
    shards, steps, velocity, modes, partner, counts, out,
    v, g_own, g_oth, total, mine, x1_src, x1_dst, corr, gathered, prefix, prior, x2_dst, mate,
    perm, load_sem, x1_send, x1_recv, x2_send, x2_recv, a_send, a_recv, b_send, b_recv,
):
    me, now = lax.axis_index("space"), lax.axis_index("tm")
    rows, times = v.shape
    half = g_own.shape[1]
    width = half // CHUNKS
    slab = rows // steps
    lower = me < shards // 2
    mirror = {"space": lax.rem(me + shards // 2, shards)}
    own_at = pl.multiple_of(jnp.where(lower, 0, half), half)
    oth_at = pl.multiple_of(jnp.where(lower, half, 0), half)

    def peer(d):
        return lax.rem(now + d, steps)

    loads = [
        pltpu.make_async_copy(velocity, v, load_sem.at[0]),
        pltpu.make_async_copy(modes.at[:, pl.ds(oth_at, half)], g_oth, load_sem.at[1]),
        pltpu.make_async_copy(modes.at[:, pl.ds(own_at, half)], g_own, load_sem.at[2]),
    ]
    for load in loads:
        load.start()

    barrier = pltpu.get_barrier_semaphore()
    pl.semaphore_signal(barrier, inc=1, device_id=mirror, device_id_type=MESH)
    for d in range(1, steps):
        pl.semaphore_signal(barrier, inc=1, device_id={"tm": peer(d)}, device_id_type=MESH)

    places = lax.broadcasted_iota(jnp.int32, (rows, rows), 0)
    hit = jnp.where((partner[...] & (rows - 1)) == places, 1.0, 0.0).astype(F32)
    perm[...] = hit.T.astype(BF16)
    sign = jnp.where(lower, 1.0, -1.0).astype(F32)

    loads[0].wait()
    loads[1].wait()
    x1, x2 = [], []
    for k in range(CHUNKS):
        cols = pl.ds(k * width, width)
        x1_src[k] = jnp.dot(v[...], g_oth[:, cols], preferred_element_type=F32).astype(BF16)
        if k == 0:
            pl.semaphore_wait(barrier, steps)
        copy = pltpu.make_async_remote_copy(
            src_ref=x1_src.at[k], dst_ref=x1_dst.at[k], send_sem=x1_send.at[k],
            recv_sem=x1_recv.at[k], device_id=mirror, device_id_type=MESH,
        )
        copy.start()
        x1.append(copy)
    loads[2].wait()
    mine[...] = jnp.dot(v[...], g_own[...], preferred_element_type=F32)

    def to_owner(k, d):
        owner = peer(d)
        return pltpu.make_async_remote_copy(
            src_ref=corr.at[k, pl.ds(owner * slab, slab)], dst_ref=gathered.at[k, now],
            send_sem=a_send.at[k, d - 1], recv_sem=a_recv.at[k, d - 1],
            device_id={"tm": owner}, device_id_type=MESH,
        )

    def from_owner(k, d):
        target = peer(d)
        return pltpu.make_async_remote_copy(
            src_ref=prefix.at[k, target],
            dst_ref=prior.at[pl.ds(now * slab, slab), pl.ds(k * width, width)],
            send_sem=b_send.at[k, d - 1], recv_sem=b_recv.at[k, d - 1],
            device_id={"tm": target}, device_id_type=MESH,
        )

    for k in range(CHUNKS):
        x1[k].wait_recv()
        theirs = jnp.dot(perm[...], x1_dst[k], preferred_element_type=F32)
        corr[k] = (mine[:, k * width : (k + 1) * width] + sign * theirs).astype(BF16)

        @pl.loop(1, steps)
        def _(d):
            to_owner(k, d).start()

    for k in range(CHUNKS):
        own_rows = pl.ds(now * slab, slab)
        gathered[k, now] = corr[k, own_rows]

        @pl.loop(1, steps)
        def _(d):
            to_owner(k, d).wait_recv()

        running = jnp.zeros((slab, width), F32)
        for j in range(steps):
            prefix[k, j] = running.astype(BF16)
            if j < steps - 1:
                running = running + gathered[k, j].astype(F32)
        prior[own_rows, k * width : (k + 1) * width] = prefix[k, now]

        @pl.loop(1, steps)
        def _(d):
            from_owner(k, d).start()

    for k in range(CHUNKS):

        @pl.loop(1, steps)
        def _(d):
            from_owner(k, d).wait_recv()

        copy = pltpu.make_async_remote_copy(
            src_ref=prior.at[:, pl.ds(k * width, width)], dst_ref=x2_dst.at[k],
            send_sem=x2_send.at[k], recv_sem=x2_recv.at[k], device_id=mirror, device_id_type=MESH,
        )
        copy.start()
        x2.append(copy)

    @pl.loop(0, times // TILE)
    def _(i):
        at = pl.ds(pl.multiple_of(i * TILE, TILE), TILE)
        total[:, at] = lax.dot_general(
            prior[...], g_own[at, :], CONTRACT_LAST, preferred_element_type=F32
        )

    for k in range(CHUNKS):
        x2[k].wait_recv()
        turned = jnp.dot(perm[...], x2_dst[k], preferred_element_type=F32)
        mate[:, k * width : (k + 1) * width] = (-sign * turned).astype(BF16)

    scale = 0.5 / counts[0].astype(F32)

    @pl.loop(0, times // TILE)
    def _(i):
        at = pl.ds(pl.multiple_of(i * TILE, TILE), TILE)
        mirrored = lax.dot_general(
            mate[...], g_oth[at, :], CONTRACT_LAST, preferred_element_type=F32
        )
        combined = (total[:, at] + mirrored) * scale
        out[:, at] = (v[:, at].astype(F32) - combined).astype(out.dtype)

    for k in range(CHUNKS):
        x1[k].wait_send()
        x2[k].wait_send()

        @pl.loop(1, steps)
        def _(d):
            to_owner(k, d).wait_send()
            from_owner(k, d).wait_send()


def solution(mesh):
    shards, steps = mesh.shape["space"], mesh.shape["tm"]

    def on_device(velocity, pressure_modes, partner, counts):
        rows, times = velocity.shape
        half = pressure_modes.shape[1] // 2
        width = half // CHUNKS
        slab = rows // steps
        dma = pltpu.SemaphoreType.DMA
        return pl.pallas_call(
            functools.partial(kernel, shards, steps),
            out_shape=jax.ShapeDtypeStruct((rows, times), BF16),
            in_specs=[
                pl.BlockSpec(memory_space=pl.ANY),
                pl.BlockSpec(memory_space=pl.ANY),
                pl.BlockSpec(memory_space=pltpu.VMEM),
                pl.BlockSpec(memory_space=pltpu.SMEM),
            ],
            out_specs=pl.BlockSpec(memory_space=pltpu.VMEM),
            scratch_shapes=[
                pltpu.VMEM((rows, times), BF16),
                pltpu.VMEM((times, half), BF16),
                pltpu.VMEM((times, half), BF16),
                pltpu.VMEM((rows, times), F32),
                pltpu.VMEM((rows, half), F32),
                pltpu.VMEM((CHUNKS, rows, width), BF16),
                pltpu.VMEM((CHUNKS, rows, width), BF16),
                pltpu.VMEM((CHUNKS, rows, width), BF16),
                pltpu.VMEM((CHUNKS, steps, slab, width), BF16),
                pltpu.VMEM((CHUNKS, steps, slab, width), BF16),
                pltpu.VMEM((rows, half), BF16),
                pltpu.VMEM((CHUNKS, rows, width), BF16),
                pltpu.VMEM((rows, half), BF16),
                pltpu.VMEM((rows, rows), BF16),
                dma((3,)),
                dma((CHUNKS,)), dma((CHUNKS,)), dma((CHUNKS,)), dma((CHUNKS,)),
                dma((CHUNKS, steps - 1)), dma((CHUNKS, steps - 1)),
                dma((CHUNKS, steps - 1)), dma((CHUNKS, steps - 1)),
            ],
            compiler_params=pltpu.CompilerParams(
                collective_id=0, has_side_effects=True, vmem_limit_bytes=48 << 20
            ),
        )(velocity, pressure_modes, partner.reshape(1, rows), counts)

    placed = (P("space", "tm"), P("tm", None), P("space"), P("tm"))
    return jax.shard_map(
        on_device, mesh=mesh, in_specs=placed, out_specs=P("space", "tm"), check_vma=False
    )
```

```python
import functools

import jax
import jax.numpy as jnp
from jax import lax
from jax.experimental import pallas as pl
from jax.experimental.pallas import tpu as pltpu
from jax.sharding import PartitionSpec as P

MESH = pl.DeviceIdType.MESH
F32, BF16 = jnp.float32, jnp.bfloat16
CHUNKS = 4
TILE = 256
CONTRACT_LAST = (((1,), (1,)), ((), ()))


def kernel(
    shards, steps, velocity, modes, partner, counts, out,
    v, g_own, g_oth, pairs, total, mine, cross_src, side_src, cross_in, diag_in, side_in,
    first, pair_sum, gathered, prefix, prior, side_prior, mate_in, turned, hit, hit_t,
    load_sem, p1_send, p1_recv, a_send, a_recv, b_send, b_recv, p2_send, p2_recv,
):
    me, now = lax.axis_index("space"), lax.axis_index("tm")
    rows, times = v.shape
    half = mine.shape[1]
    part = rows // CHUNKS
    depth = steps // 2
    slab = part // depth
    z, y = now // 2, lax.rem(now, 2)
    lower = me < shards // 2
    mirror = lax.rem(me + shards // 2, shards)
    twin = now + 1 - 2 * y
    cross, side, diag = {"space": mirror}, {"tm": twin}, {"space": mirror, "tm": twin}
    own_at = jnp.where(lower, 0, 2 * half)
    oth_at = jnp.where(lower, 2 * half, 0)

    def along(d):
        return lax.rem(z + d, depth)

    def modes_at(at):
        return modes.at[:, pl.ds(pl.multiple_of(at, half), half)]

    loads = [
        pltpu.make_async_copy(partner, pairs, load_sem.at[0]),
        pltpu.make_async_copy(velocity, v, load_sem.at[1]),
        pltpu.make_async_copy(modes_at(oth_at), g_oth.at[0], load_sem.at[2]),
        pltpu.make_async_copy(modes_at(oth_at + half), g_oth.at[1], load_sem.at[3]),
        pltpu.make_async_copy(modes_at(own_at), g_own.at[0], load_sem.at[4]),
        pltpu.make_async_copy(modes_at(own_at + half), g_own.at[1], load_sem.at[5]),
    ]
    for load in loads:
        load.start()

    barrier = pltpu.get_barrier_semaphore()
    for device in (cross, side, diag):
        pl.semaphore_signal(barrier, inc=1, device_id=device, device_id_type=MESH)
    for d in range(1, depth):
        pl.semaphore_signal(
            barrier, inc=1, device_id={"tm": 2 * along(d) + y}, device_id_type=MESH
        )

    loads[0].wait()
    places = lax.broadcasted_iota(jnp.int32, (rows, rows), 0)
    found = jnp.where((pairs[...] & (rows - 1)) == places, 1.0, 0.0).astype(F32)
    hit[...] = found.astype(BF16)
    sign = jnp.where(lower, 1.0, -1.0).astype(F32)

    def send(src, dst, sems, k, device):
        return pltpu.make_async_remote_copy(
            src_ref=src, dst_ref=dst, send_sem=sems[0].at[k], recv_sem=sems[1].at[k],
            device_id=device, device_id_type=MESH,
        )

    def lines(c):
        return pl.ds(c * part, part)

    p1, p2 = (p1_send, p1_recv), (p2_send, p2_recv)
    to_cross = [
        send(cross_src.at[y, lines(c)], cross_in.at[lines(c)], p1, 3 * c, cross)
        for c in range(CHUNKS)
    ]
    to_diag = [
        send(cross_src.at[1 - y, lines(c)], diag_in.at[lines(c)], p1, 3 * c + 1, diag)
        for c in range(CHUNKS)
    ]
    to_side = [
        send(side_src.at[lines(c)], side_in.at[lines(c)], p1, 3 * c + 2, side)
        for c in range(CHUNKS)
    ]
    back_cross = [
        send(prior.at[y, lines(c)], mate_in.at[y, lines(c)], p2, 3 * c, cross)
        for c in range(CHUNKS)
    ]
    back_diag = [
        send(prior.at[1 - y, lines(c)], mate_in.at[y, lines(c)], p2, 3 * c + 1, diag)
        for c in range(CHUNKS)
    ]
    back_side = [
        send(prior.at[1 - y, lines(c)], side_prior.at[lines(c)], p2, 3 * c + 2, side)
        for c in range(CHUNKS)
    ]

    def to_owner(c, d):
        owner = along(d)
        return pltpu.make_async_remote_copy(
            src_ref=pair_sum.at[pl.ds(c * part + owner * slab, slab)],
            dst_ref=gathered.at[c, z],
            send_sem=a_send.at[c, d - 1], recv_sem=a_recv.at[c, d - 1],
            device_id={"tm": 2 * owner + y}, device_id_type=MESH,
        )

    def from_owner(c, d):
        target = along(d)
        return pltpu.make_async_remote_copy(
            src_ref=prefix.at[c, target],
            dst_ref=prior.at[0, pl.ds(c * part + z * slab, slab)],
            send_sem=b_send.at[c, d - 1], recv_sem=b_recv.at[c, d - 1],
            device_id={"tm": 2 * target + y}, device_id_type=MESH,
        )

    loads[1].wait()
    for h in range(2):
        loads[2 + h].wait()
        product = jnp.dot(v[...], g_oth[h], preferred_element_type=F32).astype(BF16)
        cross_src[h] = jnp.dot(hit[...], product, preferred_element_type=F32).astype(BF16)
    pl.semaphore_wait(barrier, depth + 2)
    for c in range(CHUNKS):
        to_cross[c].start()
        to_diag[c].start()
    loads[4].wait()
    loads[5].wait()
    side_src[...] = jnp.dot(v[...], g_own[1 - y], preferred_element_type=F32).astype(BF16)
    for c in range(CHUNKS):
        to_side[c].start()
    mine[...] = jnp.dot(v[...], g_own[y], preferred_element_type=F32)
    hit_t[...] = found.T.astype(BF16)

    def join(c):
        to_side[c].wait_recv()
        to_cross[c].wait_recv()
        to_diag[c].wait_recv()
        here = mine[lines(c)] + sign * cross_in[lines(c)].astype(F32)
        there = side_in[lines(c)].astype(F32) + sign * diag_in[lines(c)].astype(F32)
        first[lines(c)] = jnp.where(y == 0, here, there)
        pair_sum[lines(c)] = (here + there).astype(BF16)

        @pl.loop(1, depth)
        def _(d):
            to_owner(c, d).start()

    def scan(c):
        own = pl.ds(c * part + z * slab, slab)
        gathered[c, z] = pair_sum[own]

        @pl.loop(1, depth)
        def _(d):
            to_owner(c, d).wait_recv()

        running = jnp.zeros((slab, half), F32)
        for j in range(depth):
            prefix[c, j] = running.astype(BF16)
            if j < depth - 1:
                running = running + gathered[c, j].astype(F32)
        prior[0, own] = prefix[c, z]

        @pl.loop(1, depth)
        def _(d):
            from_owner(c, d).start()

    def spread(c):
        @pl.loop(1, depth)
        def _(d):
            from_owner(c, d).wait_recv()

        prior[1, lines(c)] = (prior[0, lines(c)].astype(F32) + first[lines(c)]).astype(BF16)
        back_cross[c].start()
        back_diag[c].start()
        back_side[c].start()

    for t in range(CHUNKS + 3):
        if t < CHUNKS:
            join(t)
        if 0 <= t - 1 < CHUNKS:
            scan(t - 1)
        if 0 <= t - 2 < CHUNKS:
            spread(t - 2)

    def predicted(rows_of, modes_of, i):
        at = pl.ds(pl.multiple_of(i * TILE, TILE), TILE)
        return lax.dot_general(rows_of, modes_of[at, :], CONTRACT_LAST, preferred_element_type=F32)

    for c in range(CHUNKS):
        back_side[c].wait_recv()

    @pl.loop(0, times // TILE)
    def _(i):
        at = pl.ds(pl.multiple_of(i * TILE, TILE), TILE)
        total[:, at] = predicted(prior[y], g_own.at[y], i) + predicted(
            side_prior[...], g_own.at[1 - y], i
        )

    for c in range(CHUNKS):
        back_cross[c].wait_recv()
        back_diag[c].wait_recv()
    for h in range(2):
        moved = jnp.dot(hit_t[...], mate_in[h], preferred_element_type=F32)
        turned[h] = (-sign * moved).astype(BF16)

    scale = 0.5 / counts[0].astype(F32)

    @pl.loop(0, times // TILE)
    def _(i):
        at = pl.ds(pl.multiple_of(i * TILE, TILE), TILE)
        mirrored = predicted(turned[0], g_oth.at[0], i) + predicted(turned[1], g_oth.at[1], i)
        combined = (total[:, at] + mirrored) * scale
        out[:, at] = (v[:, at].astype(F32) - combined).astype(out.dtype)

    for c in range(CHUNKS):
        for copy in (to_cross, to_diag, to_side, back_cross, back_diag, back_side):
            copy[c].wait_send()

        @pl.loop(1, depth)
        def _(d):
            to_owner(c, d).wait_send()
            from_owner(c, d).wait_send()


def solution(mesh):
    shards, steps = mesh.shape["space"], mesh.shape["tm"]

    def on_device(velocity, pressure_modes, partner, counts):
        rows, times = velocity.shape
        half = pressure_modes.shape[1] // 4
        depth = steps // 2
        slab = rows // CHUNKS // depth
        dma = pltpu.SemaphoreType.DMA
        return pl.pallas_call(
            functools.partial(kernel, shards, steps),
            out_shape=jax.ShapeDtypeStruct((rows, times), BF16),
            in_specs=[
                pl.BlockSpec(memory_space=pltpu.HBM),
                pl.BlockSpec(memory_space=pltpu.HBM),
                pl.BlockSpec(memory_space=pltpu.HBM),
                pl.BlockSpec(memory_space=pltpu.SMEM),
            ],
            out_specs=pl.BlockSpec(memory_space=pltpu.VMEM),
            scratch_shapes=[
                pltpu.VMEM((rows, times), BF16),
                pltpu.VMEM((2, times, half), BF16),
                pltpu.VMEM((2, times, half), BF16),
                pltpu.VMEM((1, rows), jnp.int32),
                pltpu.VMEM((rows, times), F32),
                pltpu.VMEM((rows, half), F32),
                pltpu.VMEM((2, rows, half), BF16),
                pltpu.VMEM((rows, half), BF16),
                pltpu.VMEM((rows, half), BF16),
                pltpu.VMEM((rows, half), BF16),
                pltpu.VMEM((rows, half), BF16),
                pltpu.VMEM((rows, half), F32),
                pltpu.VMEM((rows, half), BF16),
                pltpu.VMEM((CHUNKS, depth, slab, half), BF16),
                pltpu.VMEM((CHUNKS, depth, slab, half), BF16),
                pltpu.VMEM((2, rows, half), BF16),
                pltpu.VMEM((rows, half), BF16),
                pltpu.VMEM((2, rows, half), BF16),
                pltpu.VMEM((2, rows, half), BF16),
                pltpu.VMEM((rows, rows), BF16),
                pltpu.VMEM((rows, rows), BF16),
                dma((6,)),
                dma((3 * CHUNKS,)), dma((3 * CHUNKS,)),
                dma((CHUNKS, depth - 1)), dma((CHUNKS, depth - 1)),
                dma((CHUNKS, depth - 1)), dma((CHUNKS, depth - 1)),
                dma((3 * CHUNKS,)), dma((3 * CHUNKS,)),
            ],
            compiler_params=pltpu.CompilerParams(
                collective_id=0, has_side_effects=True, vmem_limit_bytes=48 << 20
            ),
        )(velocity, pressure_modes, partner.reshape(1, rows), counts)

    placed = (P("space", "tm"), P("tm", None), P("space"), P("tm"))
    return jax.shard_map(
        on_device, mesh=mesh, in_specs=placed, out_specs=P("space", "tm"), check_vma=False
    )
```

```python
import functools

import jax
import jax.numpy as jnp
from jax import lax
from jax.experimental import pallas as pl
from jax.experimental.pallas import tpu as pltpu
from jax.sharding import PartitionSpec as P

MESH = pl.DeviceIdType.MESH
F32, BF16 = jnp.float32, jnp.bfloat16
CHUNKS = 4
TILE = 256
ORDER = (
    (0, 0), (0, 1), (0, 2), (1, 0), (0, 3), (1, 1),
    (1, 2), (2, 0), (1, 3), (2, 1), (2, 2), (2, 3),
)
CONTRACT_LAST = (((1,), (1,)), ((), ()))


def kernel(
    shards, steps, velocity, modes, partner, counts, out,
    v, g_own, g_oth, pairs, total, mine, cross_src, side_src, cross_in, diag_in, side_in,
    g_oth_t, first, pair_sum, gathered, prefix, prior, side_prior, mate_in, turned, hit, hit_t,
    load_sem, p1_send, p1_recv, a_send, a_recv, b_send, b_recv, p2_send, p2_recv,
):
    me, now = lax.axis_index("space"), lax.axis_index("tm")
    rows, times = v.shape
    half = mine.shape[1]
    part = rows // CHUNKS
    depth = steps // 2
    slab = part // depth
    z, y = now // 2, lax.rem(now, 2)
    lower = me < shards // 2
    mirror = lax.rem(me + shards // 2, shards)
    twin = now + 1 - 2 * y
    cross, side, diag = {"space": mirror}, {"tm": twin}, {"space": mirror, "tm": twin}
    own_at = jnp.where(lower, 0, 2 * half)
    oth_at = jnp.where(lower, 2 * half, 0)

    def along(d):
        return lax.rem(z + d, depth)

    def modes_at(at):
        return modes.at[:, pl.ds(pl.multiple_of(at, half), half)]

    loads = [
        pltpu.make_async_copy(partner, pairs, load_sem.at[0]),
        pltpu.make_async_copy(velocity, v, load_sem.at[1]),
        pltpu.make_async_copy(modes_at(oth_at + (1 - y) * half), g_oth.at[1 - y], load_sem.at[2]),
        pltpu.make_async_copy(modes_at(oth_at + y * half), g_oth.at[y], load_sem.at[3]),
        pltpu.make_async_copy(modes_at(own_at + (1 - y) * half), g_own.at[1 - y], load_sem.at[4]),
        pltpu.make_async_copy(modes_at(own_at + y * half), g_own.at[y], load_sem.at[5]),
    ]
    for load in loads:
        load.start()

    barrier = pltpu.get_barrier_semaphore()
    for device in (cross, side, diag):
        pl.semaphore_signal(barrier, inc=1, device_id=device, device_id_type=MESH)
    for d in range(1, depth):
        pl.semaphore_signal(
            barrier, inc=1, device_id={"tm": 2 * along(d) + y}, device_id_type=MESH
        )

    loads[0].wait()
    places = lax.broadcasted_iota(jnp.int32, (rows, rows), 0)
    found = jnp.where((pairs[...] & (rows - 1)) == places, 1.0, 0.0).astype(F32)
    hit[...] = found.astype(BF16)
    sign = jnp.where(lower, 1.0, -1.0).astype(F32)

    def send(src, dst, sems, k, device):
        return pltpu.make_async_remote_copy(
            src_ref=src, dst_ref=dst, send_sem=sems[0].at[k], recv_sem=sems[1].at[k],
            device_id=device, device_id_type=MESH,
        )

    def lines(c):
        return pl.ds(c * part, part)

    p1, p2 = (p1_send, p1_recv), (p2_send, p2_recv)
    to_cross = [
        send(cross_src.at[y, lines(c)], cross_in.at[lines(c)], p1, 3 * c, cross)
        for c in range(CHUNKS)
    ]
    to_diag = [
        send(cross_src.at[1 - y, lines(c)], diag_in.at[lines(c)], p1, 3 * c + 1, diag)
        for c in range(CHUNKS)
    ]
    to_side = [
        send(side_src.at[lines(c)], side_in.at[lines(c)], p1, 3 * c + 2, side)
        for c in range(CHUNKS)
    ]
    back_cross = [
        send(prior.at[y, lines(c)], mate_in.at[y, lines(c)], p2, 3 * c, cross)
        for c in range(CHUNKS)
    ]
    back_diag = [
        send(prior.at[1 - y, lines(c)], mate_in.at[y, lines(c)], p2, 3 * c + 1, diag)
        for c in range(CHUNKS)
    ]
    back_side = [
        send(prior.at[1 - y, lines(c)], side_prior.at[lines(c)], p2, 3 * c + 2, side)
        for c in range(CHUNKS)
    ]

    def to_owner(c, d):
        owner = along(d)
        return pltpu.make_async_remote_copy(
            src_ref=pair_sum.at[pl.ds(c * part + owner * slab, slab)],
            dst_ref=gathered.at[c, z],
            send_sem=a_send.at[c, d - 1], recv_sem=a_recv.at[c, d - 1],
            device_id={"tm": 2 * owner + y}, device_id_type=MESH,
        )

    def from_owner(c, d):
        target = along(d)
        return pltpu.make_async_remote_copy(
            src_ref=prefix.at[c, target],
            dst_ref=prior.at[0, pl.ds(c * part + z * slab, slab)],
            send_sem=b_send.at[c, d - 1], recv_sem=b_recv.at[c, d - 1],
            device_id={"tm": 2 * target + y}, device_id_type=MESH,
        )

    loads[1].wait()
    for load, h in ((loads[2], 1 - y), (loads[3], y)):
        load.wait()
        product = jnp.dot(v[...], g_oth[h], preferred_element_type=F32).astype(BF16)
        cross_src[h] = jnp.dot(hit[...], product, preferred_element_type=F32).astype(BF16)
        if load is loads[2]:
            pl.semaphore_wait(barrier, depth + 2)
            to_diag[0].start()
            to_diag[1].start()
    to_cross[0].start()
    to_cross[1].start()
    for c in range(2, CHUNKS):
        to_diag[c].start()
        to_cross[c].start()
    loads[4].wait()
    side_src[...] = jnp.dot(v[...], g_own[1 - y], preferred_element_type=F32).astype(BF16)
    for c in range(CHUNKS):
        to_side[c].start()
    loads[5].wait()
    mine[...] = jnp.dot(v[...], g_own[y], preferred_element_type=F32)
    hit_t[...] = found.T.astype(BF16)

    @pl.loop(0, times // TILE)
    def _(i):
        at = pl.ds(pl.multiple_of(i * TILE, TILE), TILE)
        for h in range(2):
            g_oth_t[h, :, at] = g_oth[h, at, :].T

    def join(c):
        to_side[c].wait_recv()
        to_cross[c].wait_recv()
        to_diag[c].wait_recv()
        here = mine[lines(c)] + sign * cross_in[lines(c)].astype(F32)
        there = side_in[lines(c)].astype(F32) + sign * diag_in[lines(c)].astype(F32)
        first[lines(c)] = jnp.where(y == 0, here, there)
        pair_sum[lines(c)] = (here + there).astype(BF16)

        for d in range(1, depth):
            to_owner(c, d).start()

    def scan(c):
        own = pl.ds(c * part + z * slab, slab)
        gathered[c, z] = pair_sum[own]

        for d in range(1, depth):
            to_owner(c, d).wait_recv()

        running = jnp.zeros((slab, half), F32)
        for j in range(depth):
            prefix[c, j] = running.astype(BF16)
            if j < depth - 1:
                running = running + gathered[c, j].astype(F32)
        prior[0, own] = prefix[c, z]

        for d in range(1, depth):
            from_owner(c, d).start()

    def spread(c):
        for d in range(1, depth):
            from_owner(c, d).wait_recv()

        prior[1, lines(c)] = (prior[0, lines(c)].astype(F32) + first[lines(c)]).astype(BF16)
        back_side[c].start()
        back_diag[c].start()
        back_cross[c].start()

    stages = [join, scan, spread]
    for stage, c in ORDER:
        stages[stage](c)

    def predicted(rows_of, modes_of, i):
        at = pl.ds(pl.multiple_of(i * TILE, TILE), TILE)
        return lax.dot_general(rows_of, modes_of[at, :], CONTRACT_LAST, preferred_element_type=F32)

    def arrived(some):
        for c in some:
            back_diag[c].wait_recv()
            back_cross[c].wait_recv()
        span = slice(some[0] * part, (some[-1] + 1) * part)
        return [
            -sign * jnp.dot(hit_t[:, span], mate_in[h, span], preferred_element_type=F32)
            for h in range(2)
        ]

    @pl.loop(0, times // TILE)
    def _(i):
        at = pl.ds(pl.multiple_of(i * TILE, TILE), TILE)
        total[:, at] = predicted(prior[y], g_own.at[y], i)

    early = arrived(range(CHUNKS // 2))
    for h in range(2):
        turned[h] = early[h].astype(BF16)
    for c in range(CHUNKS):
        back_side[c].wait_recv()

    @pl.loop(0, times // TILE)
    def _(i):
        at = pl.ds(pl.multiple_of(i * TILE, TILE), TILE)
        total[:, at] += predicted(side_prior[...], g_own.at[1 - y], i)

    late = arrived(range(CHUNKS // 2, CHUNKS))
    for h in range(2):
        turned[h] = (turned[h].astype(F32) + late[h]).astype(BF16)

    scale = 0.5 / counts[0].astype(F32)

    @pl.loop(0, times // TILE)
    def _(i):
        at = pl.ds(pl.multiple_of(i * TILE, TILE), TILE)
        mirrored = jnp.dot(turned[0], g_oth_t[0, :, at], preferred_element_type=F32) + jnp.dot(
            turned[1], g_oth_t[1, :, at], preferred_element_type=F32
        )
        combined = (total[:, at] + mirrored) * scale
        out[:, at] = (v[:, at].astype(F32) - combined).astype(out.dtype)

    for c in range(CHUNKS):
        for copy in (to_cross, to_diag, to_side, back_cross, back_diag, back_side):
            copy[c].wait_send()

        @pl.loop(1, depth)
        def _(d):
            to_owner(c, d).wait_send()
            from_owner(c, d).wait_send()


def solution(mesh):
    shards, steps = mesh.shape["space"], mesh.shape["tm"]

    def on_device(velocity, pressure_modes, partner, counts):
        rows, times = velocity.shape
        half = pressure_modes.shape[1] // 4
        depth = steps // 2
        slab = rows // CHUNKS // depth
        dma = pltpu.SemaphoreType.DMA

        def in_hbm(array):
            return pltpu.with_memory_space_constraint(array, pltpu.HBM)

        return pl.pallas_call(
            functools.partial(kernel, shards, steps),
            out_shape=jax.ShapeDtypeStruct((rows, times), BF16),
            in_specs=[
                pl.BlockSpec(memory_space=pltpu.HBM),
                pl.BlockSpec(memory_space=pltpu.HBM),
                pl.BlockSpec(memory_space=pltpu.HBM),
                pl.BlockSpec(memory_space=pltpu.SMEM),
            ],
            out_specs=pl.BlockSpec(memory_space=pltpu.VMEM),
            scratch_shapes=[
                pltpu.VMEM((rows, times), BF16),
                pltpu.VMEM((2, times, half), BF16),
                pltpu.VMEM((2, times, half), BF16),
                pltpu.VMEM((1, rows), jnp.int32),
                pltpu.VMEM((rows, times), F32),
                pltpu.VMEM((rows, half), F32),
                pltpu.VMEM((2, rows, half), BF16),
                pltpu.VMEM((rows, half), BF16),
                pltpu.VMEM((rows, half), BF16),
                pltpu.VMEM((rows, half), BF16),
                pltpu.VMEM((rows, half), BF16),
                pltpu.VMEM((2, half, times), BF16),
                pltpu.VMEM((rows, half), F32),
                pltpu.VMEM((rows, half), BF16),
                pltpu.VMEM((CHUNKS, depth, slab, half), BF16),
                pltpu.VMEM((CHUNKS, depth, slab, half), BF16),
                pltpu.VMEM((2, rows, half), BF16),
                pltpu.VMEM((rows, half), BF16),
                pltpu.VMEM((2, rows, half), BF16),
                pltpu.VMEM((2, rows, half), BF16),
                pltpu.VMEM((rows, rows), BF16),
                pltpu.VMEM((rows, rows), BF16),
                dma((6,)),
                dma((3 * CHUNKS,)), dma((3 * CHUNKS,)),
                dma((CHUNKS, depth - 1)), dma((CHUNKS, depth - 1)),
                dma((CHUNKS, depth - 1)), dma((CHUNKS, depth - 1)),
                dma((3 * CHUNKS,)), dma((3 * CHUNKS,)),
            ],
            compiler_params=pltpu.CompilerParams(
                collective_id=0, has_side_effects=True, vmem_limit_bytes=48 << 20
            ),
        )(*map(in_hbm, (velocity, pressure_modes, partner.reshape(1, rows))), counts)

    placed = (P("space", "tm"), P("tm", None), P("space"), P("tm"))
    return jax.shard_map(
        on_device, mesh=mesh, in_specs=placed, out_specs=P("space", "tm"), check_vma=False
    )
```

```python
import functools

import jax
import jax.numpy as jnp
from jax import lax
from jax.experimental import pallas as pl
from jax.experimental.pallas import tpu as pltpu
from jax.sharding import PartitionSpec as P

MESH = pl.DeviceIdType.MESH
F32, BF16 = jnp.float32, jnp.bfloat16
TILE = 256
PIECES = 4
CUTS = 2
CHUNKS = 4 * CUTS
ORDER = sorted(((s, c) for s in range(3) for c in range(CHUNKS)), key=lambda e: e[1] + 3.9 * e[0])
CONTRACT_LAST = (((1,), (1,)), ((), ()))


def kernel(
    shards, steps, velocity, modes, partner, counts, out,
    v, g_own, g_oth, pairs, total, mine, cross_src, side_src, cross_in, diag_in, side_in,
    g_oth_t, first, pair_sum, gathered, prefix, prior, side_prior, mate_in, turned, hit, hit_t,
    load_sem, p1_send, p1_recv, a_send, a_recv, b_send, b_recv, p2_send, p2_recv,
):
    me, now = lax.axis_index("space"), lax.axis_index("tm")
    rows, times = v.shape
    half = mine.shape[1]
    part, width = rows // (CHUNKS // CUTS), half // CUTS
    depth = steps // 2
    slab = part // depth
    z, y = now // 2, lax.rem(now, 2)
    lower = me < shards // 2
    mirror = lax.rem(me + shards // 2, shards)
    twin = now + 1 - 2 * y
    cross, side, diag = {"space": mirror}, {"tm": twin}, {"space": mirror, "tm": twin}
    own_at = jnp.where(lower, 0, 2 * half)
    oth_at = jnp.where(lower, 2 * half, 0)

    def along(d):
        return lax.rem(z + d, depth)

    def modes_at(at):
        return modes.at[:, pl.ds(pl.multiple_of(at, half), half)]

    loads = [
        pltpu.make_async_copy(partner, pairs, load_sem.at[0]),
        pltpu.make_async_copy(modes_at(oth_at + y * half), g_oth.at[y], load_sem.at[1]),
        pltpu.make_async_copy(modes_at(own_at + (1 - y) * half), g_own.at[1 - y], load_sem.at[2]),
        pltpu.make_async_copy(modes_at(own_at + y * half), g_own.at[y], load_sem.at[3]),
    ]
    piece = times // PIECES
    diag_at = pl.ds(pl.multiple_of(oth_at + (1 - y) * half, half), half)
    pieces = []
    for i in range(PIECES):
        at = pl.ds(i * piece, piece)
        pieces.append((
            pltpu.make_async_copy(velocity.at[:, at], v.at[:, at], load_sem.at[4 + 2 * i]),
            pltpu.make_async_copy(
                modes.at[at, diag_at], g_oth.at[1 - y, at], load_sem.at[5 + 2 * i]
            ),
        ))
    loads[0].start()
    for pair in pieces:
        for load in pair:
            load.start()
    for load in loads[1:]:
        load.start()

    barrier = pltpu.get_barrier_semaphore()
    for device in (cross, side, diag):
        pl.semaphore_signal(barrier, inc=1, device_id=device, device_id_type=MESH)
    for d in range(1, depth):
        pl.semaphore_signal(
            barrier, inc=1, device_id={"tm": 2 * along(d) + y}, device_id_type=MESH
        )

    loads[0].wait()
    places = lax.broadcasted_iota(jnp.int32, (rows, rows), 0)
    found = jnp.where((pairs[...] & (rows - 1)) == places, 1.0, 0.0).astype(F32)
    hit[...] = found.astype(BF16)
    sign = jnp.where(lower, 1.0, -1.0).astype(F32)

    def send(src, dst, sems, k, device):
        return pltpu.make_async_remote_copy(
            src_ref=src, dst_ref=dst, send_sem=sems[0].at[k], recv_sem=sems[1].at[k],
            device_id=device, device_id_type=MESH,
        )

    def block(c):
        return pl.ds(c // CUTS * part, part), pl.ds(c % CUTS * width, width)

    def slab_of(c, owner):
        return pl.ds(c // CUTS * part + owner * slab, slab), pl.ds(c % CUTS * width, width)

    p1, p2 = (p1_send, p1_recv), (p2_send, p2_recv)
    to_cross = [
        send(cross_src.at[y, *block(c)], cross_in.at[*block(c)], p1, 3 * c, cross)
        for c in range(CHUNKS)
    ]
    to_diag = [
        send(cross_src.at[1 - y, *block(c)], diag_in.at[*block(c)], p1, 3 * c + 1, diag)
        for c in range(CHUNKS)
    ]
    to_side = [
        send(side_src.at[*block(c)], side_in.at[*block(c)], p1, 3 * c + 2, side)
        for c in range(CHUNKS)
    ]
    back_cross = [
        send(prior.at[y, *block(c)], mate_in.at[y, *block(c)], p2, 3 * c, cross)
        for c in range(CHUNKS)
    ]
    back_diag = [
        send(prior.at[1 - y, *block(c)], mate_in.at[y, *block(c)], p2, 3 * c + 1, diag)
        for c in range(CHUNKS)
    ]
    back_side = [
        send(prior.at[1 - y, *block(c)], side_prior.at[*block(c)], p2, 3 * c + 2, side)
        for c in range(CHUNKS)
    ]

    def to_owner(c, d):
        owner = along(d)
        return pltpu.make_async_remote_copy(
            src_ref=pair_sum.at[slab_of(c, owner)],
            dst_ref=gathered.at[c, z],
            send_sem=a_send.at[c, d - 1], recv_sem=a_recv.at[c, d - 1],
            device_id={"tm": 2 * owner + y}, device_id_type=MESH,
        )

    def from_owner(c, d):
        target = along(d)
        return pltpu.make_async_remote_copy(
            src_ref=prefix.at[c, target],
            dst_ref=prior.at[0, *slab_of(c, z)],
            send_sem=b_send.at[c, d - 1], recv_sem=b_recv.at[c, d - 1],
            device_id={"tm": 2 * target + y}, device_id_type=MESH,
        )

    def crossing(h, product):
        cross_src[h] = jnp.dot(hit[...], product.astype(BF16), preferred_element_type=F32).astype(BF16)

    product = jnp.zeros((rows, half), F32)
    for i, pair in enumerate(pieces):
        for load in pair:
            load.wait()
        at = pl.ds(i * piece, piece)
        product += jnp.dot(v[:, at], g_oth[1 - y, at], preferred_element_type=F32)
    crossing(1 - y, product)
    pl.semaphore_wait(barrier, depth + 2)
    for c in range(CHUNKS // 2):
        to_diag[c].start()
    loads[1].wait()
    crossing(y, jnp.dot(v[...], g_oth[y], preferred_element_type=F32))
    for c in range(CHUNKS // 2):
        to_cross[c].start()
    for c in range(CHUNKS // 2, CHUNKS):
        to_diag[c].start()
        to_cross[c].start()
    loads[2].wait()
    side_src[...] = jnp.dot(v[...], g_own[1 - y], preferred_element_type=F32).astype(BF16)
    for c in range(CHUNKS):
        to_side[c].start()
    loads[3].wait()
    mine[...] = jnp.dot(v[...], g_own[y], preferred_element_type=F32)
    hit_t[...] = found.T.astype(BF16)

    @pl.loop(0, times // TILE)
    def _(i):
        at = pl.ds(pl.multiple_of(i * TILE, TILE), TILE)
        for h in range(2):
            g_oth_t[h, :, at] = g_oth[h, at, :].T

    def join(c):
        to_side[c].wait_recv()
        to_cross[c].wait_recv()
        to_diag[c].wait_recv()
        here = mine[*block(c)] + sign * cross_in[*block(c)].astype(F32)
        there = side_in[*block(c)].astype(F32) + sign * diag_in[*block(c)].astype(F32)
        first[*block(c)] = jnp.where(y == 0, here, there)
        pair_sum[*block(c)] = (here + there).astype(BF16)

        for d in range(1, depth):
            to_owner(c, d).start()

    def scan(c):
        own = slab_of(c, z)
        gathered[c, z] = pair_sum[own]

        for d in range(1, depth):
            to_owner(c, d).wait_recv()

        running = jnp.zeros((slab, width), F32)
        for j in range(depth):
            prefix[c, j] = running.astype(BF16)
            if j < depth - 1:
                running = running + gathered[c, j].astype(F32)
        prior[0, *own] = prefix[c, z]

        for d in range(1, depth):
            from_owner(c, d).start()

    def spread(c):
        for d in range(1, depth):
            from_owner(c, d).wait_recv()

        prior[1, *block(c)] = (prior[0, *block(c)].astype(F32) + first[*block(c)]).astype(BF16)
        back_side[c].start()
        back_diag[c].start()
        back_cross[c].start()

    stages = [join, scan, spread]
    for stage, c in ORDER:
        stages[stage](c)

    def predicted(rows_of, modes_of, i):
        at = pl.ds(pl.multiple_of(i * TILE, TILE), TILE)
        return lax.dot_general(rows_of, modes_of[at, :], CONTRACT_LAST, preferred_element_type=F32)

    def arrived(some):
        for c in some:
            back_diag[c].wait_recv()
            back_cross[c].wait_recv()
        span = slice(some[0] // CUTS * part, (some[-1] // CUTS + 1) * part)
        return [
            -sign * jnp.dot(hit_t[:, span], mate_in[h, span], preferred_element_type=F32)
            for h in range(2)
        ]

    @pl.loop(0, times // TILE)
    def _(i):
        at = pl.ds(pl.multiple_of(i * TILE, TILE), TILE)
        total[:, at] = predicted(prior[y], g_own.at[y], i)

    early = arrived(range(CHUNKS // 2))
    for h in range(2):
        turned[h] = early[h].astype(BF16)
    for c in range(CHUNKS):
        back_side[c].wait_recv()

    @pl.loop(0, times // TILE)
    def _(i):
        at = pl.ds(pl.multiple_of(i * TILE, TILE), TILE)
        total[:, at] += predicted(side_prior[...], g_own.at[1 - y], i)

    late = arrived(range(CHUNKS // 2, CHUNKS))
    for h in range(2):
        turned[h] = (turned[h].astype(F32) + late[h]).astype(BF16)

    scale = 0.5 / counts[0].astype(F32)

    @pl.loop(0, times // TILE)
    def _(i):
        at = pl.ds(pl.multiple_of(i * TILE, TILE), TILE)
        mirrored = jnp.dot(turned[0], g_oth_t[0, :, at], preferred_element_type=F32) + jnp.dot(
            turned[1], g_oth_t[1, :, at], preferred_element_type=F32
        )
        combined = (total[:, at] + mirrored) * scale
        out[:, at] = (v[:, at].astype(F32) - combined).astype(out.dtype)

    for c in range(CHUNKS):
        for copy in (to_cross, to_diag, to_side, back_cross, back_diag, back_side):
            copy[c].wait_send()

        @pl.loop(1, depth)
        def _(d):
            to_owner(c, d).wait_send()
            from_owner(c, d).wait_send()


def solution(mesh):
    shards, steps = mesh.shape["space"], mesh.shape["tm"]

    def on_device(velocity, pressure_modes, partner, counts):
        rows, times = velocity.shape
        half = pressure_modes.shape[1] // 4
        depth = steps // 2
        slab = rows // (CHUNKS // CUTS) // depth
        width = half // CUTS
        dma = pltpu.SemaphoreType.DMA

        def in_hbm(array):
            return pltpu.with_memory_space_constraint(array, pltpu.HBM)

        return pl.pallas_call(
            functools.partial(kernel, shards, steps),
            out_shape=jax.ShapeDtypeStruct((rows, times), BF16),
            in_specs=[
                pl.BlockSpec(memory_space=pltpu.HBM),
                pl.BlockSpec(memory_space=pltpu.HBM),
                pl.BlockSpec(memory_space=pltpu.HBM),
                pl.BlockSpec(memory_space=pltpu.SMEM),
            ],
            out_specs=pl.BlockSpec(memory_space=pltpu.VMEM),
            scratch_shapes=[
                pltpu.VMEM((rows, times), BF16),
                pltpu.VMEM((2, times, half), BF16),
                pltpu.VMEM((2, times, half), BF16),
                pltpu.VMEM((1, rows), jnp.int32),
                pltpu.VMEM((rows, times), F32),
                pltpu.VMEM((rows, half), F32),
                pltpu.VMEM((2, rows, half), BF16),
                pltpu.VMEM((rows, half), BF16),
                pltpu.VMEM((rows, half), BF16),
                pltpu.VMEM((rows, half), BF16),
                pltpu.VMEM((rows, half), BF16),
                pltpu.VMEM((2, half, times), BF16),
                pltpu.VMEM((rows, half), F32),
                pltpu.VMEM((rows, half), BF16),
                pltpu.VMEM((CHUNKS, depth, slab, width), BF16),
                pltpu.VMEM((CHUNKS, depth, slab, width), BF16),
                pltpu.VMEM((2, rows, half), BF16),
                pltpu.VMEM((rows, half), BF16),
                pltpu.VMEM((2, rows, half), BF16),
                pltpu.VMEM((2, rows, half), BF16),
                pltpu.VMEM((rows, rows), BF16),
                pltpu.VMEM((rows, rows), BF16),
                dma((4 + 2 * PIECES,)),
                dma((3 * CHUNKS,)), dma((3 * CHUNKS,)),
                dma((CHUNKS, depth - 1)), dma((CHUNKS, depth - 1)),
                dma((CHUNKS, depth - 1)), dma((CHUNKS, depth - 1)),
                dma((3 * CHUNKS,)), dma((3 * CHUNKS,)),
            ],
            compiler_params=pltpu.CompilerParams(
                collective_id=0, has_side_effects=True, vmem_limit_bytes=48 << 20
            ),
        )(*map(in_hbm, (velocity, pressure_modes, partner.reshape(1, rows))), counts)

    placed = (P("space", "tm"), P("tm", None), P("space"), P("tm"))
    return jax.shard_map(
        on_device, mesh=mesh, in_specs=placed, out_specs=P("space", "tm"), check_vma=False
    )
```
